768 devices in a mesh: dom: 64 (over y, z_lo, core), feat: 12 (over z_hi, x).
Axes of the slice: x: 4, y: 8, z: 12 (z_hi: 3, z_lo: 4; z = z_hi * 4 + z_lo), core: 2. Of those that a mesh axis runs over, the one named last changes fastest.
Arguments:
- node_state: bfloat16 [1179648, 128], P(('dom', 'feat')), may hold values from -6 to 6
- w_msg: bfloat16 [128, 128], replicated, may hold values from -0.5 to 0.5
- w_first: bfloat16 [256, 128], replicated, may hold values from -0.375 to 0.375
- b_first: float32 [128], replicated, may hold values from -3 to 3
- w_second: bfloat16 [128, 128], replicated, may hold values from -0.5 to 0.5
- b_second: float32 [128], replicated, may hold values from -3 to 3
- ln_gain: float32 [128], replicated, may hold values from 0.5 to 1.5
- col_index: int32 [9216, 4], P(('dom', 'feat')), may hold values from 0 to 9215, as said below
- edge_counts: int32 [9216, 4, 128, 128], P(('dom', 'feat')), may hold values from 0 to 3, as said below
- cotangent: bfloat16 [1179648, 128], P(('dom', 'feat')), may hold values from -14 to 14
Outputs:
- updated: bfloat16 [1179648, 128], P(('dom', 'feat'))
- grad_state: bfloat16 [1179648, 128], P(('dom', 'feat'))
- grad_w_msg: float32 [128, 128], replicated
- grad_w_first: float32 [256, 128], replicated
- grad_b_first: float32 [128], replicated
- grad_w_second: float32 [128, 128], replicated
- grad_b_second: float32 [128], replicated
- grad_gain: float32 [128], replicated
The draws below stay inside these ranges and needn't reach their ends.
Inputs may be any that keep to these rules, and one draw needn't show every extreme that they name: `col_index`: tile 0 of block row b is block b itself; every other tile's column lies within 2 blocks of b, reflected at the two ends of the curve; columns of one block row may repeat. `edge_counts`: most entries are zero.
All inputs are finite; a program needn't handle non-finite values.
Results may differ from the reference program's by a relative error of at most 0.0093.
Values may be sent and summed in bfloat16 or wider, within the bound.
A program may use at most 32 MiB of HBM per device.

```python
import jax
import jax.numpy as jnp
from jax import lax

HID = 128
BLK = 128
TILES = 4
WIN = 2
NB_DEV = 12
NBLKS = 9216
NODES = 1179648


def draw_col_index(key, part):
    block_rows = jnp.arange(NBLKS, dtype=jnp.int32)
    offsets = jax.random.randint(key, (NBLKS, TILES - 1), -WIN, WIN + 1, dtype=jnp.int32)
    offsets = jnp.concatenate([jnp.zeros((NBLKS, 1), jnp.int32), offsets], axis=1)
    columns = block_rows[:, None] + offsets
    columns = jnp.where(columns < 0, -columns, columns)
    columns = jnp.where(columns > NBLKS - 1, 2 * (NBLKS - 1) - columns, columns)
    return columns.astype(jnp.int32)


def draw_edge_counts(key, part):
    key_live = jax.random.fold_in(key, 11)
    key_value = jax.random.fold_in(key, 23)
    shape_all = (NBLKS, TILES, BLK, BLK)
    live = jax.random.randint(key_live, shape_all, 0, BLK, dtype=jnp.int32) < 2
    values = jax.random.randint(key_value, shape_all, 1, 4, dtype=jnp.int32)
    return jnp.where(live, values, 0).astype(jnp.int32)


def draw_cotangent(key, part):
    key_base = jax.random.fold_in(key, 5)
    positions = jnp.arange(NODES, dtype=jnp.float32) / NODES
    row_scale = jnp.power(10.0, positions - 0.5)
    base = jnp.clip(jax.random.normal(key_base, (NODES, HID), jnp.float32), -4.0, 4.0)
    return (base * row_scale[:, None]).astype(jnp.bfloat16)


def level_of(own_key, extent, split, least, high):
    def one(dim, shards_of):
        heights = jax.random.uniform(jax.random.fold_in(jax.random.fold_in(own_key, 6), dim), (shards_of,), jnp.float32, least / len(split), high / len(split))
        return jnp.repeat(jnp.exp(heights), extent[dim] // shards_of).reshape((-1,) + (1,) * (len(extent) - dim - 1))

    level = one(*split[0])
    for cut in split[1:]:
        level = level * one(*cut)
    return level


def normal_values(own_key, shape, scale, limit, pieces=(), held_as=jnp.bfloat16):
    result = jax.random.normal(own_key, shape, jnp.float32) * scale
    if len(pieces) > 0:
        result = level_of(own_key, shape, pieces, -0.22, 0.18) * result
    return jnp.clip(result, min=-limit, max=limit).astype(held_as)


def setup_inputs(seed: int = 0) -> dict:
    arg_keys = jax.random.split(jax.random.key(seed), 11)
    return {
        "node_state": normal_values(arg_keys[0], (NODES, HID), 1.0, 6.0, ((0, 768),)),
        "w_msg": normal_values(arg_keys[1], (HID, HID), HID ** -0.5, 0.5),
        "w_first": normal_values(arg_keys[2], (2 * HID, HID), (2 * HID) ** -0.5, 0.375),
        "b_first": normal_values(arg_keys[3], (HID,), 0.5, 3.0, (), jnp.float32),
        "w_second": normal_values(arg_keys[4], (HID, HID), HID ** -0.5, 0.5),
        "b_second": normal_values(arg_keys[5], (HID,), 0.5, 3.0, (), jnp.float32),
        "ln_gain": jnp.clip(jax.random.uniform(arg_keys[6], (HID,), jnp.float32, 0.5, 1.5), 0.5, 1.5),
        "col_index": draw_col_index(jax.random.fold_in(arg_keys[10], 71), 0),
        "edge_counts": draw_edge_counts(jax.random.fold_in(arg_keys[10], 71), 0),
        "cotangent": draw_cotangent(jax.random.fold_in(arg_keys[10], 71), 0),
    }


epsilon = 1e-05

def inner_rows(left, right):
    return lax.dot_general(left, right, (((0,), (0,)), ((), ())), preferred_element_type=jnp.float32)

def times_transposed(left, right):
    return lax.dot_general(left, right, (((1,), (1,)), ((), ())), preferred_element_type=jnp.float32)

def reference(node_state, w_msg, w_first, b_first, w_second, b_second, ln_gain, col_index, edge_counts, cotangent):
    node_total = node_state.shape[0]
    groups = NBLKS // NB_DEV
    messages = jnp.dot(node_state, w_msg, preferred_element_type=jnp.float32).astype(jnp.bfloat16)
    msg_blocks = messages.reshape(NBLKS, BLK, HID)

    def forward_group(group_index):
        start = group_index * NB_DEV
        col_slice = lax.dynamic_slice_in_dim(col_index, start, NB_DEV, 0)
        count_slice = lax.dynamic_slice_in_dim(edge_counts, start, NB_DEV, 0).astype(jnp.float32)
        picked = msg_blocks[col_slice].astype(jnp.float32)
        return jnp.einsum('btij,btjh->bih', count_slice, picked)
    aggregate = lax.map(forward_group, jnp.arange(groups, dtype=jnp.int32))
    aggregate = aggregate.reshape(node_total, HID).astype(jnp.bfloat16)
    joined = jnp.concatenate([node_state, aggregate], axis=1)
    pre_hidden = jnp.dot(joined, w_first, preferred_element_type=jnp.float32) + b_first
    activated = jax.nn.silu(pre_hidden).astype(jnp.bfloat16)
    pre_norm = jnp.dot(activated, w_second, preferred_element_type=jnp.float32) + b_second
    row_mean = lax.optimization_barrier(jnp.mean(pre_norm, axis=-1, keepdims=True))
    centred = pre_norm - row_mean
    inv_std = lax.rsqrt(lax.optimization_barrier(jnp.mean(centred * centred, axis=-1, keepdims=True)) + epsilon)
    normed = centred * inv_std
    updated = (node_state.astype(jnp.float32) + ln_gain * normed).astype(jnp.bfloat16)
    cot_f32 = cotangent.astype(jnp.float32)
    d_normed = cot_f32 * ln_gain
    d_pre_norm = (inv_std * (d_normed - lax.optimization_barrier(jnp.mean(d_normed, axis=-1, keepdims=True)) - normed * lax.optimization_barrier(jnp.mean(d_normed * normed, axis=-1, keepdims=True)))).astype(jnp.bfloat16)
    sigmoid_z = jax.nn.sigmoid(pre_hidden)
    d_pre_hidden = (times_transposed(d_pre_norm, w_second) * sigmoid_z * (1.0 + pre_hidden * (1.0 - sigmoid_z))).astype(jnp.bfloat16)
    d_joined = times_transposed(d_pre_hidden, w_first)
    d_aggregate = d_joined[:, HID:].astype(jnp.bfloat16).reshape(NBLKS, BLK, HID)
    span_blocks = NB_DEV + 2 * WIN

    def backward_group(group_index):
        start = jnp.clip(group_index * NB_DEV - WIN, 0, NBLKS - span_blocks).astype(jnp.int32)
        col_slice = lax.dynamic_slice_in_dim(col_index, start, span_blocks, 0)
        count_slice = lax.dynamic_slice_in_dim(edge_counts, start, span_blocks, 0).astype(jnp.float32)
        grad_slice = lax.dynamic_slice_in_dim(d_aggregate, start, span_blocks, 0).astype(jnp.float32)
        contribution = jnp.einsum('btij,bih->btjh', count_slice, grad_slice)
        one_hot = ((col_slice - group_index * NB_DEV)[:, :, None] == jnp.arange(NB_DEV, dtype=jnp.int32)[None, None, :]).astype(jnp.float32)
        return jnp.einsum('btc,btjh->cjh', one_hot, contribution, precision=lax.Precision.HIGHEST)
    d_messages = lax.map(backward_group, jnp.arange(groups, dtype=jnp.int32))
    d_messages = d_messages.reshape(node_total, HID).astype(jnp.bfloat16)
    grad_state = (cot_f32 + d_joined[:, :HID] + times_transposed(d_messages, w_msg)).astype(jnp.bfloat16)
    grad_scale = 1.0 / jnp.sqrt(jnp.float32(NODES))
    grad_w_msg = inner_rows(node_state, d_messages) * grad_scale
    grad_w_first = inner_rows(joined, d_pre_hidden) * grad_scale
    grad_b_first = lax.optimization_barrier(jnp.sum(d_pre_hidden.astype(jnp.float32), axis=0)) * grad_scale
    grad_w_second = inner_rows(activated, d_pre_norm) * grad_scale
    grad_b_second = lax.optimization_barrier(jnp.sum(d_pre_norm.astype(jnp.float32), axis=0)) * grad_scale
    grad_gain = lax.optimization_barrier(jnp.sum(cot_f32 * normed, axis=0)) * grad_scale
    return (updated, grad_state, grad_w_msg, grad_w_first, grad_b_first, grad_w_second, grad_b_second, grad_gain)
```

```python
import functools
import math

import jax
import jax.numpy as jnp
from jax import lax
from jax.experimental import pallas as pl
from jax.experimental.pallas import tpu as pltpu
from jax.sharding import PartitionSpec as P

MESH = pl.DeviceIdType.MESH
WIN = 2
SPAN = 2 * WIN + 1
EPS = 1e-05
NX, NY, NZ, Z_LO, CORES = 4, 8, 12, 4, 2
PIECE = 8
QUARTER = PIECE * NY
HALF = QUARTER * NX
TOTAL = HALF * CORES
GROUP = 2


def dot(a, b):
    return jnp.dot(a, b, preferred_element_type=jnp.float32)


def dot_rt(a, b):
    return lax.dot_general(a, b, (((1,), (1,)), ((), ())), preferred_element_type=jnp.float32)


def dot_lt(a, b):
    return lax.dot_general(a, b, (((0,), (0,)), ((), ())), preferred_element_type=jnp.float32)


def layer_kernel(
    x_hbm, wmsg_hbm, wf_hbm, bf_hbm, ws_hbm, bs_hbm, gain_hbm, col_hbm, cnt_hbm, cot_hbm,
    upd_out, gs_out, tot_out,
    xe, wmsg, wf, bf, ws, bs, gain, col, cnt, cot,
    band, dag, gsp, dme, pay, r1, a1, r2, a2, r3, a3, r4, out, bh_send, bh_recv,
    in_sem, cnt_sem, halo_s, halo_r, c_s, c_r, x_s, x_r, y_s, y_r, z_s, z_r,
    ay_s, ay_r, ax_s, ax_r, ac_s, ac_r, b_s, b_r,
):
    nb = cnt_hbm.shape[0]
    rows = x_hbm.shape[0]
    blk = cnt_hbm.shape[2]
    edge = WIN * blk
    ndom, nfeat = lax.axis_size("dom"), lax.axis_size("feat")
    count = ndom * nfeat
    dom, feat = lax.axis_index("dom"), lax.axis_index("feat")
    core, z_lo, y = lax.rem(dom, CORES), lax.rem(dom // CORES, Z_LO), dom // (CORES * Z_LO)
    x, z_hi = lax.rem(feat, NX), feat // NX
    z = z_hi * Z_LO + z_lo
    rank = dom * nfeat + feat
    first_block = rank * nb

    def by_rank(r):
        return (r // nfeat, lax.rem(r, nfeat))

    nxt = by_rank(lax.rem(rank + 1, count))
    prv = by_rank(lax.rem(rank + count - 1, count))
    mate = (dom + 1 - 2 * core, feat)

    def at_x(k):
        return (dom, z_hi * NX + lax.rem(x + k, NX))

    def at_y(k):
        return ((lax.rem(y + k, NY) * Z_LO + z_lo) * CORES + core, feat)

    def at_z(k):
        other = lax.rem(z + k, NZ)
        return ((y * Z_LO + lax.rem(other, Z_LO)) * CORES + core, (other // Z_LO) * NX + x)

    peers = [prv, nxt]
    peers += [at_z(k) for k in (6, 5, 7, 4, 8, 3, 9, 2, 10, 1, 11)]
    peers += [at_y(k) for k in range(1, NY)]
    peers += [at_x(k) for k in range(1, NX)]
    peers += [mate]
    barrier = pltpu.get_barrier_semaphore()
    for peer in peers:
        pl.semaphore_signal(barrier, inc=1, device_id=peer, device_id_type=MESH)

    loads = [
        pltpu.make_async_copy(src, dst, in_sem.at[i])
        for i, (src, dst) in enumerate(
            (
                (col_hbm, col),
                (x_hbm, xe.at[pl.ds(edge, rows)]),
                (cot_hbm, cot),
                (wmsg_hbm, wmsg),
                (wf_hbm, wf),
                (bf_hbm, bf),
                (ws_hbm, ws),
                (bs_hbm, bs),
                (gain_hbm, gain),
            )
        )
    ]
    cnt_loads = [pltpu.make_async_copy(cnt_hbm.at[b], cnt.at[b], cnt_sem.at[b]) for b in range(nb)]
    loads[0].start()
    for b in range(nb):
        cnt_loads[b].start()
    for load in loads[1:]:
        load.start()

    pay[...] = jnp.zeros_like(pay)
    dme[...] = jnp.zeros_like(dme)
    loads[0].wait()

    def build(b, carry):
        pltpu.make_async_copy(cnt_hbm.at[b], cnt.at[b], cnt_sem.at[b]).wait()
        tiles = [cnt[b, t].astype(jnp.float32).astype(jnp.bfloat16) for t in range(cnt.shape[1])]
        for d in range(SPAN):
            acc = tiles[0] if d == WIN else None
            for t in range(1, cnt.shape[1]):
                here = (col[b, t] - first_block - b + WIN == d).astype(jnp.float32)
                term = tiles[t] * jnp.full((blk, blk), here, jnp.float32).astype(jnp.bfloat16)
                acc = term if acc is None else acc + term
            band[b, :, d * blk : (d + 1) * blk] = acc
        return carry

    lax.fori_loop(0, nb, build, 0)
    pl.semaphore_wait(barrier, len(peers))

    halo_low = pltpu.make_async_remote_copy(
        src_ref=x_hbm.at[pl.ds(0, edge)], dst_ref=xe.at[pl.ds(edge + rows, edge)],
        send_sem=halo_s.at[0], recv_sem=halo_r.at[0], device_id=prv, device_id_type=MESH,
    )
    halo_high = pltpu.make_async_remote_copy(
        src_ref=x_hbm.at[pl.ds(rows - edge, edge)], dst_ref=xe.at[pl.ds(0, edge)],
        send_sem=halo_s.at[1], recv_sem=halo_r.at[1], device_id=nxt, device_id_type=MESH,
    )
    halo_low.start()
    halo_high.start()
    for load in loads[1:]:
        load.wait()

    size = GROUP * blk

    def process(b0):
        r0 = pl.multiple_of(b0 * blk, blk)
        here = pl.ds(r0, size)
        xs = xe[pl.ds(r0 + edge, size), :]
        agx = jnp.concatenate(
            [dot(band[b0 + g], xe[pl.ds(r0 + g * blk, SPAN * blk), :]) for g in range(GROUP)], axis=0
        ).astype(jnp.bfloat16)
        agg = dot(agx, wmsg[...]).astype(jnp.bfloat16)
        ph = dot(jnp.concatenate([xs, agg], axis=1), wf[...]) + bf[...]
        sg = jax.nn.sigmoid(ph)
        act = (ph * sg).astype(jnp.bfloat16)
        pn = dot(act, ws[...]) + bs[...]
        cen = pn - jnp.mean(pn, axis=-1, keepdims=True)
        inv = lax.rsqrt(jnp.mean(cen * cen, axis=-1, keepdims=True) + EPS)
        nrm = cen * inv
        upd_out[here, :] = (xs.astype(jnp.float32) + gain[...] * nrm).astype(jnp.bfloat16)
        c = cot[here, :].astype(jnp.float32)
        q = c * gain[...]
        dpn = (
            inv
            * (
                q
                - jnp.mean(q, axis=-1, keepdims=True)
                - nrm * jnp.mean(q * nrm, axis=-1, keepdims=True)
            )
        ).astype(jnp.bfloat16)
        dph = (dot_rt(dpn, ws[...]) * sg * (1.0 + ph * (1.0 - sg))).astype(jnp.bfloat16)
        dj = dot_rt(dph, wf[...])
        gsp[here, :] = c + dj[:, :blk]
        dag[here, :] = dj[:, blk:].astype(jnp.bfloat16)
        g1 = dot_lt(dph, jnp.concatenate([xs, agx], axis=1))
        pay[0:blk, :] += g1[:, :blk]
        pay[blk : 2 * blk, :] += g1[:, blk:]
        pay[2 * blk : 3 * blk, :] += dot_lt(act, dpn)
        pay[3 * blk : 3 * blk + 1, :] += jnp.sum(dph.astype(jnp.float32), axis=0, keepdims=True)
        pay[3 * blk + 1 : 3 * blk + 2, :] += jnp.sum(dpn.astype(jnp.float32), axis=0, keepdims=True)
        pay[3 * blk + 2 : 3 * blk + 3, :] += jnp.sum(c * nrm, axis=0, keepdims=True)

    def interior(i, carry):
        process(WIN + GROUP * i)
        return carry

    lax.fori_loop(0, (nb - 2 * WIN) // GROUP, interior, 0)
    halo_low.wait_recv()
    halo_high.wait_recv()

    def border(i, carry):
        process(i * (nb - WIN))
        return carry

    lax.fori_loop(0, 2, border, 0)

    order = (2, 1, 3, 0)
    quarters = [lax.rem(x + off, NX) for off in order]
    to_mate = []
    for j, q in enumerate(quarters):
        to_mate.append(
            pltpu.make_async_remote_copy(
                src_ref=pay.at[pl.ds(pl.multiple_of((1 - core) * HALF + q * QUARTER, PIECE), QUARTER)],
                dst_ref=r1.at[j], send_sem=c_s.at[j], recv_sem=c_r.at[j], device_id=mate, device_id_type=MESH,
            )
        )
        to_mate[-1].start()

    def scatter_row(b):
        r0 = pl.multiple_of(b * blk, blk)
        dme[pl.ds(r0, SPAN * blk), :] += dot_lt(band[b], dag[pl.ds(r0, blk), :])

    sends = list(to_mate)
    along_x = []
    for j, q in enumerate(quarters):
        to_mate[j].wait_recv()
        mine = pay[pl.ds(pl.multiple_of(core * HALF + q * QUARTER, PIECE), QUARTER), :]
        a1[j] = mine + r1[j]
        off = order[j]
        if off:
            copy = pltpu.make_async_remote_copy(
                src_ref=a1.at[j], dst_ref=r2.at[j],
                send_sem=x_s.at[j], recv_sem=x_r.at[j], device_id=at_x(off), device_id_type=MESH,
            )
            copy.start()
            along_x.append(copy)
    sends += along_x

    def border_rows(i, carry):
        b0 = i * (nb - WIN)
        for g in range(WIN):
            scatter_row(b0 + g)
        return carry

    lax.fori_loop(0, 2, border_rows, 0)
    bh_send[0] = dme[0:edge, :].astype(jnp.bfloat16)
    bh_send[1] = dme[edge + rows : 2 * edge + rows, :].astype(jnp.bfloat16)
    back_low = pltpu.make_async_remote_copy(
        src_ref=bh_send.at[0], dst_ref=bh_recv.at[0],
        send_sem=b_s.at[0], recv_sem=b_r.at[0], device_id=prv, device_id_type=MESH,
    )
    back_high = pltpu.make_async_remote_copy(
        src_ref=bh_send.at[1], dst_ref=bh_recv.at[1],
        send_sem=b_s.at[1], recv_sem=b_r.at[1], device_id=nxt, device_id_type=MESH,
    )
    back_low.start()
    back_high.start()
    sends += [halo_low, halo_high, back_low, back_high]

    for copy in along_x:
        copy.wait_recv()
    a2[...] = (a1[3] + r2[0]) + (r2[1] + r2[2])
    along_y = []
    for k in range(1, NY):
        copy = pltpu.make_async_remote_copy(
            src_ref=a2.at[pl.ds(pl.multiple_of(lax.rem(y + k, NY) * PIECE, PIECE), PIECE)],
            dst_ref=r3.at[k - 1],
            send_sem=y_s.at[k - 1], recv_sem=y_r.at[k - 1], device_id=at_y(k), device_id_type=MESH,
        )
        copy.start()
        along_y.append(copy)
    sends += along_y

    def inner_rows(b, carry):
        scatter_row(b)
        return carry

    lax.fori_loop(WIN, nb - WIN, inner_rows, 0)

    for copy in along_y:
        copy.wait_recv()
    total = a2[pl.ds(pl.multiple_of(y * PIECE, PIECE), PIECE), :]
    for k in range(1, NY):
        total = total + r3[k - 1]
    a3[...] = total
    r4[z] = total
    along_z = []
    for k in (6, 5, 7, 4, 8, 3, 9, 2, 10, 1, 11):
        copy = pltpu.make_async_remote_copy(
            src_ref=a3, dst_ref=r4.at[z],
            send_sem=z_s.at[k - 1], recv_sem=z_r.at[k - 1], device_id=at_z(k), device_id_type=MESH,
        )
        copy.start()
        along_z.append(copy)
    sends += along_z

    back_low.wait_recv()
    back_high.wait_recv()
    dme[edge : 2 * edge, :] += bh_recv[1].astype(jnp.float32)
    dme[rows : rows + edge, :] += bh_recv[0].astype(jnp.float32)

    def state_rows(i, carry):
        r0 = pl.multiple_of(i * size, size)
        here = pl.ds(r0, size)
        dm = dme[pl.ds(r0 + edge, size), :].astype(jnp.bfloat16)
        gs_out[here, :] = (gsp[here, :] + dot_rt(dm, wmsg[...])).astype(jnp.bfloat16)
        return carry

    lax.fori_loop(0, rows // size, state_rows, 0)

    for copy in along_z:
        copy.wait_recv()
    total = r4[0]
    for i in range(1, NZ):
        total = total + r4[i]
    half0 = core * HALF
    quarter0 = half0 + x * QUARTER
    own = pl.ds(pl.multiple_of(quarter0 + y * PIECE, PIECE), PIECE)
    out[own, :] = total
    gathers = []
    for k in range(1, NY):
        copy = pltpu.make_async_remote_copy(
            src_ref=out.at[own], dst_ref=out.at[own],
            send_sem=ay_s.at[k - 1], recv_sem=ay_r.at[k - 1], device_id=at_y(k), device_id_type=MESH,
        )
        copy.start()
        gathers.append(copy)
    for copy in gathers:
        copy.wait_recv()
    sends += gathers
    span = pl.ds(pl.multiple_of(quarter0, QUARTER), QUARTER)
    along_x = []
    for j, k in enumerate((2, 1, 3)):
        copy = pltpu.make_async_remote_copy(
            src_ref=out.at[span], dst_ref=out.at[span],
            send_sem=ax_s.at[j], recv_sem=ax_r.at[j], device_id=at_x(k), device_id_type=MESH,
        )
        copy.start()
        along_x.append(copy)
    sends += along_x
    shares = []
    for j, k in enumerate((0, 1, 3, 2)):
        if k:
            along_x[(2, 1, 3).index(k)].wait_recv()
        span = pl.ds(pl.multiple_of(half0 + lax.rem(x + NX - k, NX) * QUARTER, QUARTER), QUARTER)
        copy = pltpu.make_async_remote_copy(
            src_ref=out.at[span], dst_ref=out.at[span],
            send_sem=ac_s.at[j], recv_sem=ac_r.at[j], device_id=mate, device_id_type=MESH,
        )
        copy.start()
        shares.append(copy)
    sends += shares
    for copy in shares:
        copy.wait_recv()
    tot_out[...] = out[...]
    for copy in sends:
        copy.wait_send()


def finish_kernel(scale, upd_in, gs_in, tot, wmsg, wf, upd, gs, gwm, gwf, gb1, gws, gb2, gg):
    n = wmsg.shape[0]
    upd[...] = upd_in[...]
    gs[...] = gs_in[...]
    high = lax.Precision.HIGHEST
    s_t = tot[n : 2 * n, :]
    s = s_t.T
    low = wf[n:, :].astype(jnp.float32)
    gwm[...] = scale * lax.dot_general(
        s, low, (((1,), (1,)), ((), ())), precision=high, preferred_element_type=jnp.float32
    )
    gwf[0:n, :] = scale * tot[0:n, :].T
    gwf[n:, :] = scale * jnp.dot(
        wmsg[...].astype(jnp.float32).T, s, precision=high, preferred_element_type=jnp.float32
    )
    gws[...] = scale * tot[2 * n : 3 * n, :]
    gb1[...] = scale * tot[3 * n : 3 * n + 1, :]
    gb2[...] = scale * tot[3 * n + 1 : 3 * n + 2, :]
    gg[...] = scale * tot[3 * n + 2 : 3 * n + 3, :]


def shards(
    node_state, w_msg, w_first, b_first, w_second, b_second, ln_gain, col_index, edge_counts, cotangent
):
    rows, hid = node_state.shape
    nb, tiles, blk, _ = edge_counts.shape
    ext = rows + 2 * WIN * blk
    devices = lax.axis_size("dom") * lax.axis_size("feat")
    scale = 1.0 / math.sqrt(rows * devices)
    f32, bf16 = jnp.float32, jnp.bfloat16
    vmem, sem = pltpu.VMEM, pltpu.SemaphoreType.DMA
    anywhere = pl.BlockSpec(memory_space=pl.ANY)
    whole = pl.BlockSpec(memory_space=pltpu.VMEM)
    shape = jax.ShapeDtypeStruct
    upd, gs, tot = pl.pallas_call(
        layer_kernel,
        out_shape=(shape((rows, hid), bf16), shape((rows, hid), bf16), shape((TOTAL, hid), f32)),
        in_specs=[anywhere] * 10,
        out_specs=(whole,) * 3,
        scratch_shapes=[
            vmem((ext, hid), bf16), vmem((hid, hid), bf16), vmem((2 * hid, hid), bf16), vmem((1, hid), f32),
            vmem((hid, hid), bf16), vmem((1, hid), f32), vmem((1, hid), f32), pltpu.SMEM((nb, tiles), jnp.int32),
            vmem((nb, tiles, blk, blk), jnp.int32), vmem((rows, hid), bf16),
            vmem((nb, blk, SPAN * blk), bf16), vmem((rows, hid), bf16), vmem((rows, hid), f32), vmem((ext, hid), f32),
            vmem((TOTAL, hid), f32), vmem((NX, QUARTER, hid), f32), vmem((NX, QUARTER, hid), f32),
            vmem((NX - 1, QUARTER, hid), f32), vmem((QUARTER, hid), f32), vmem((NY - 1, PIECE, hid), f32),
            vmem((PIECE, hid), f32), vmem((NZ, PIECE, hid), f32), vmem((TOTAL, hid), f32),
            vmem((2, WIN * blk, hid), bf16), vmem((2, WIN * blk, hid), bf16),
            sem((9,)), sem((nb,)), sem((2,)), sem((2,)), sem((4,)), sem((4,)), sem((3,)), sem((3,)),
            sem((7,)), sem((7,)), sem((11,)), sem((11,)), sem((7,)), sem((7,)), sem((3,)), sem((3,)),
            sem((4,)), sem((4,)), sem((2,)), sem((2,)),
        ],
        compiler_params=pltpu.CompilerParams(
            collective_id=0, has_side_effects=True, vmem_limit_bytes=48 * 1024 * 1024
        ),
        name="layer",
    )(
        node_state, w_msg, w_first, b_first.reshape(1, hid), w_second, b_second.reshape(1, hid),
        ln_gain.reshape(1, hid), col_index, edge_counts, cotangent,
    )
    row = shape((1, hid), f32)
    upd, gs, gwm, gwf, gb1, gws, gb2, gg = pl.pallas_call(
        functools.partial(finish_kernel, scale),
        out_shape=(
            shape((rows, hid), bf16), shape((rows, hid), bf16), shape((hid, hid), f32),
            shape((2 * hid, hid), f32), row, shape((hid, hid), f32), row, row,
        ),
        in_specs=[whole] * 5,
        out_specs=(whole,) * 8,
        name="finish",
    )(upd, gs, tot, w_msg, w_first)
    return (upd, gs, gwm, gwf, gb1.reshape(hid), gws, gb2.reshape(hid), gg.reshape(hid))


def solution(mesh):
    nodes = P(("dom", "feat"), None)
    return jax.shard_map(
        shards,
        mesh=mesh,
        in_specs=(nodes, P(), P(), P(), P(), P(), P(), nodes, P(("dom", "feat"), None, None, None), nodes),
        out_specs=(nodes, nodes, P(), P(), P(), P(), P(), P()),
        check_vma=False,
    )
```

```python
import functools
import math

import jax
import jax.numpy as jnp
from jax import lax
from jax.experimental import pallas as pl
from jax.experimental.pallas import tpu as pltpu
from jax.sharding import PartitionSpec as P

MESH = pl.DeviceIdType.MESH
WIN = 2
SPAN = 2 * WIN + 1
EPS = 1e-05
NX, NY, NZ, Z_LO, CORES = 4, 8, 12, 4, 2
PIECE = 8
QUARTER = PIECE * NY
HALF = QUARTER * NX
TOTAL = HALF * CORES
GROUP = 2


def dot(a, b):
    return jnp.dot(a, b, preferred_element_type=jnp.float32)


def dot_rt(a, b):
    return lax.dot_general(a, b, (((1,), (1,)), ((), ())), preferred_element_type=jnp.float32)


def dot_lt(a, b):
    return lax.dot_general(a, b, (((0,), (0,)), ((), ())), preferred_element_type=jnp.float32)


def layer_kernel(
    scale,
    x_hbm, wmsg_hbm, wf_hbm, bf_hbm, ws_hbm, bs_hbm, gain_hbm, col_hbm, cnt_hbm, cot_hbm,
    upd_out, gs_out, gwm_out, gwf_out, gb1_out, gws_out, gb2_out, gg_out,
    xe, wmsg, wmsg_t, wf, bf, ws, bs, gain, col, cnt, cot,
    band, dag, gsp, dme, pay, r1, a1, r2, a2, r3, a3, r4, out, bh_send, bh_recv,
    in_sem, cnt_sem, halo_s, halo_r, c_s, c_r, x_s, x_r, y_s, y_r, z_s, z_r,
    ay_s, ay_r, ax_s, ax_r, ac_s, ac_r, b_s, b_r,
):
    nb = cnt_hbm.shape[0]
    hid = x_hbm.shape[1]
    rows = x_hbm.shape[0]
    blk = cnt_hbm.shape[2]
    edge = WIN * blk
    ndom, nfeat = lax.axis_size("dom"), lax.axis_size("feat")
    count = ndom * nfeat
    dom, feat = lax.axis_index("dom"), lax.axis_index("feat")
    core, z_lo, y = lax.rem(dom, CORES), lax.rem(dom // CORES, Z_LO), dom // (CORES * Z_LO)
    x, z_hi = lax.rem(feat, NX), feat // NX
    z = z_hi * Z_LO + z_lo
    rank = dom * nfeat + feat
    first_block = rank * nb

    def by_rank(r):
        return (r // nfeat, lax.rem(r, nfeat))

    nxt = by_rank(lax.rem(rank + 1, count))
    prv = by_rank(lax.rem(rank + count - 1, count))
    mate = (dom + 1 - 2 * core, feat)

    def at_x(k):
        return (dom, z_hi * NX + lax.rem(x + k, NX))

    def at_y(k):
        return ((lax.rem(y + k, NY) * Z_LO + z_lo) * CORES + core, feat)

    def at_z(k):
        other = lax.rem(z + k, NZ)
        return ((y * Z_LO + lax.rem(other, Z_LO)) * CORES + core, (other // Z_LO) * NX + x)

    peers = [prv, nxt]
    peers += [at_z(k) for k in (6, 5, 7, 4, 8, 3, 9, 2, 10, 1, 11)]
    peers += [at_y(k) for k in range(1, NY)]
    peers += [at_x(k) for k in range(1, NX)]
    peers += [mate]
    barrier = pltpu.get_barrier_semaphore()
    for peer in peers:
        pl.semaphore_signal(barrier, inc=1, device_id=peer, device_id_type=MESH)

    loads = [
        pltpu.make_async_copy(src, dst, in_sem.at[i])
        for i, (src, dst) in enumerate(
            (
                (col_hbm, col),
                (x_hbm, xe.at[pl.ds(edge, rows)]),
                (cot_hbm, cot),
                (wmsg_hbm, wmsg),
                (wf_hbm, wf),
                (bf_hbm, bf),
                (ws_hbm, ws),
                (bs_hbm, bs),
                (gain_hbm, gain),
            )
        )
    ]
    cnt_loads = [pltpu.make_async_copy(cnt_hbm.at[b], cnt.at[b], cnt_sem.at[b]) for b in range(nb)]
    loads[0].start()
    for b in range(nb):
        cnt_loads[b].start()
    for load in loads[1:]:
        load.start()

    pay[...] = jnp.zeros_like(pay)
    dme[...] = jnp.zeros_like(dme)
    loads[0].wait()

    def build(b, carry):
        pltpu.make_async_copy(cnt_hbm.at[b], cnt.at[b], cnt_sem.at[b]).wait()
        tiles = [cnt[b, t].astype(jnp.float32).astype(jnp.bfloat16) for t in range(cnt.shape[1])]
        for d in range(SPAN):
            acc = tiles[0] if d == WIN else None
            for t in range(1, cnt.shape[1]):
                here = (col[t, b] - first_block - b + WIN == d).astype(jnp.float32)
                term = tiles[t] * jnp.full((blk, blk), here, jnp.float32).astype(jnp.bfloat16)
                acc = term if acc is None else acc + term
            band[b, :, d * blk : (d + 1) * blk] = acc
        return carry

    lax.fori_loop(0, nb, build, 0)
    pl.semaphore_wait(barrier, len(peers))

    halo_low = pltpu.make_async_remote_copy(
        src_ref=x_hbm.at[pl.ds(0, edge)], dst_ref=xe.at[pl.ds(edge + rows, edge)],
        send_sem=halo_s.at[0], recv_sem=halo_r.at[0], device_id=prv, device_id_type=MESH,
    )
    halo_high = pltpu.make_async_remote_copy(
        src_ref=x_hbm.at[pl.ds(rows - edge, edge)], dst_ref=xe.at[pl.ds(0, edge)],
        send_sem=halo_s.at[1], recv_sem=halo_r.at[1], device_id=nxt, device_id_type=MESH,
    )
    halo_low.start()
    halo_high.start()
    for load in loads[1:]:
        load.wait()

    wmsg_t[...] = wmsg[...].T
    size = GROUP * blk

    def process(b0):
        r0 = pl.multiple_of(b0 * blk, blk)
        here = pl.ds(r0, size)
        xs = xe[pl.ds(r0 + edge, size), :]
        agx = jnp.concatenate(
            [dot(band[b0 + g], xe[pl.ds(r0 + g * blk, SPAN * blk), :]) for g in range(GROUP)], axis=0
        ).astype(jnp.bfloat16)
        agg = dot(agx, wmsg[...]).astype(jnp.bfloat16)
        ph = dot(jnp.concatenate([xs, agg], axis=1), wf[...]) + bf[...]
        sg = jax.nn.sigmoid(ph)
        act = (ph * sg).astype(jnp.bfloat16)
        pn = dot(act, ws[...]) + bs[...]
        cen = pn - jnp.mean(pn, axis=-1, keepdims=True)
        inv = lax.rsqrt(jnp.mean(cen * cen, axis=-1, keepdims=True) + EPS)
        nrm = cen * inv
        upd_out[here, :] = (xs.astype(jnp.float32) + gain[...] * nrm).astype(jnp.bfloat16)
        c = cot[here, :].astype(jnp.float32)
        q = c * gain[...]
        dpn = (
            inv
            * (
                q
                - jnp.mean(q, axis=-1, keepdims=True)
                - nrm * jnp.mean(q * nrm, axis=-1, keepdims=True)
            )
        ).astype(jnp.bfloat16)
        dph = (dot_rt(dpn, ws[...]) * sg * (1.0 + ph * (1.0 - sg))).astype(jnp.bfloat16)
        dj = dot_rt(dph, wf[...])
        gsp[here, :] = c + dj[:, :blk]
        dag[here, :] = dj[:, blk:].astype(jnp.bfloat16)
        pay[0:blk, :] += dot_lt(xs, dph)
        pay[blk : 2 * blk, :] += dot_lt(agx, dph)
        pay[2 * blk : 3 * blk, :] += dot_lt(act, dpn)
        pay[3 * blk : 3 * blk + 1, :] += jnp.sum(dph.astype(jnp.float32), axis=0, keepdims=True)
        pay[3 * blk + 1 : 3 * blk + 2, :] += jnp.sum(dpn.astype(jnp.float32), axis=0, keepdims=True)
        pay[3 * blk + 2 : 3 * blk + 3, :] += jnp.sum(c * nrm, axis=0, keepdims=True)

    def interior(i, carry):
        process(WIN + GROUP * i)
        return carry

    lax.fori_loop(0, (nb - 2 * WIN) // GROUP, interior, 0)
    halo_low.wait_recv()
    halo_high.wait_recv()

    def border(i, carry):
        process(i * (nb - WIN))
        return carry

    lax.fori_loop(0, 2, border, 0)

    order = (2, 1, 3, 0)
    quarters = [lax.rem(x + off, NX) for off in order]
    to_mate = []
    for j, q in enumerate(quarters):
        to_mate.append(
            pltpu.make_async_remote_copy(
                src_ref=pay.at[pl.ds(pl.multiple_of((1 - core) * HALF + q * QUARTER, PIECE), QUARTER)],
                dst_ref=r1.at[j], send_sem=c_s.at[j], recv_sem=c_r.at[j], device_id=mate, device_id_type=MESH,
            )
        )
        to_mate[-1].start()

    def scatter_row(b):
        r0 = pl.multiple_of(b * blk, blk)
        dme[pl.ds(r0, SPAN * blk), :] += dot_lt(band[b], dag[pl.ds(r0, blk), :])

    sends = list(to_mate)
    along_x = []
    for j, q in enumerate(quarters):
        to_mate[j].wait_recv()
        mine = pay[pl.ds(pl.multiple_of(core * HALF + q * QUARTER, PIECE), QUARTER), :]
        a1[j] = mine + r1[j]
        off = order[j]
        if off:
            copy = pltpu.make_async_remote_copy(
                src_ref=a1.at[j], dst_ref=r2.at[j],
                send_sem=x_s.at[j], recv_sem=x_r.at[j], device_id=at_x(off), device_id_type=MESH,
            )
            copy.start()
            along_x.append(copy)
    sends += along_x

    def border_rows(i, carry):
        b0 = i * (nb - WIN)
        for g in range(WIN):
            scatter_row(b0 + g)
        return carry

    lax.fori_loop(0, 2, border_rows, 0)
    bh_send[0] = dme[0:edge, :].astype(jnp.bfloat16)
    bh_send[1] = dme[edge + rows : 2 * edge + rows, :].astype(jnp.bfloat16)
    back_low = pltpu.make_async_remote_copy(
        src_ref=bh_send.at[0], dst_ref=bh_recv.at[0],
        send_sem=b_s.at[0], recv_sem=b_r.at[0], device_id=prv, device_id_type=MESH,
    )
    back_high = pltpu.make_async_remote_copy(
        src_ref=bh_send.at[1], dst_ref=bh_recv.at[1],
        send_sem=b_s.at[1], recv_sem=b_r.at[1], device_id=nxt, device_id_type=MESH,
    )
    back_low.start()
    back_high.start()
    sends += [halo_low, halo_high, back_low, back_high]

    for copy in along_x:
        copy.wait_recv()
    a2[...] = (a1[3] + r2[0]) + (r2[1] + r2[2])
    along_y = []
    for k in range(1, NY):
        copy = pltpu.make_async_remote_copy(
            src_ref=a2.at[pl.ds(pl.multiple_of(lax.rem(y + k, NY) * PIECE, PIECE), PIECE)],
            dst_ref=r3.at[k - 1],
            send_sem=y_s.at[k - 1], recv_sem=y_r.at[k - 1], device_id=at_y(k), device_id_type=MESH,
        )
        copy.start()
        along_y.append(copy)
    sends += along_y

    def inner_rows(b, carry):
        scatter_row(b)
        return carry

    lax.fori_loop(WIN, nb - WIN, inner_rows, 0)

    for copy in along_y:
        copy.wait_recv()
    total = a2[pl.ds(pl.multiple_of(y * PIECE, PIECE), PIECE), :]
    for k in range(1, NY):
        total = total + r3[k - 1]
    total = total * scale
    a3[...] = total
    r4[z] = total
    along_z = []
    for k in (6, 5, 7, 4, 8, 3, 9, 2, 10, 1, 11):
        copy = pltpu.make_async_remote_copy(
            src_ref=a3, dst_ref=r4.at[z],
            send_sem=z_s.at[k - 1], recv_sem=z_r.at[k - 1], device_id=at_z(k), device_id_type=MESH,
        )
        copy.start()
        along_z.append(copy)
    sends += along_z

    back_low.wait_recv()
    back_high.wait_recv()
    dme[edge : 2 * edge, :] += bh_recv[1].astype(jnp.float32)
    dme[rows : rows + edge, :] += bh_recv[0].astype(jnp.float32)

    def state_rows(i, carry):
        r0 = pl.multiple_of(i * size, size)
        here = pl.ds(r0, size)
        dm = dme[pl.ds(r0 + edge, size), :].astype(jnp.bfloat16)
        gs_out[here, :] = (gsp[here, :] + dot_rt(dm, wmsg[...])).astype(jnp.bfloat16)
        return carry

    lax.fori_loop(0, rows // size, state_rows, 0)

    for copy in along_z:
        copy.wait_recv()
    total = r4[0]
    for i in range(1, NZ):
        total = total + r4[i]
    half0 = core * HALF
    quarter0 = half0 + x * QUARTER
    own = pl.ds(pl.multiple_of(quarter0 + y * PIECE, PIECE), PIECE)
    out[own, :] = total
    gathers = []
    for k in range(1, NY):
        copy = pltpu.make_async_remote_copy(
            src_ref=out.at[own], dst_ref=out.at[own],
            send_sem=ay_s.at[k - 1], recv_sem=ay_r.at[k - 1], device_id=at_y(k), device_id_type=MESH,
        )
        copy.start()
        gathers.append(copy)
    for copy in gathers:
        copy.wait_recv()
    sends += gathers
    span = pl.ds(pl.multiple_of(quarter0, QUARTER), QUARTER)
    along_x = []
    for j, k in enumerate((2, 1, 3)):
        copy = pltpu.make_async_remote_copy(
            src_ref=out.at[span], dst_ref=out.at[span],
            send_sem=ax_s.at[j], recv_sem=ax_r.at[j], device_id=at_x(k), device_id_type=MESH,
        )
        copy.start()
        along_x.append(copy)
    sends += along_x
    shares = []
    for j, k in enumerate((0, 1, 3, 2)):
        if k:
            along_x[(2, 1, 3).index(k)].wait_recv()
        span = pl.ds(pl.multiple_of(half0 + lax.rem(x + NX - k, NX) * QUARTER, QUARTER), QUARTER)
        copy = pltpu.make_async_remote_copy(
            src_ref=out.at[span], dst_ref=out.at[span],
            send_sem=ac_s.at[j], recv_sem=ac_r.at[j], device_id=mate, device_id_type=MESH,
        )
        copy.start()
        shares.append(copy)
    sends += shares
    for copy in shares:
        copy.wait_recv()
    grad_s = out[hid : 2 * hid, :]
    part1 = grad_s.astype(jnp.bfloat16)
    rest = grad_s - part1.astype(jnp.float32)
    part2 = rest.astype(jnp.bfloat16)
    part3 = (rest - part2.astype(jnp.float32)).astype(jnp.bfloat16)
    low = wf[hid:, :]
    gwm_out[...] = (dot_rt(part3, low) + dot_rt(part2, low)) + dot_rt(part1, low)
    gwf_out[0:hid, :] = out[0:hid, :]
    turned = wmsg_t[...]
    gwf_out[hid:, :] = (dot(turned, part3) + dot(turned, part2)) + dot(turned, part1)
    gws_out[...] = out[2 * hid : 3 * hid, :]
    gb1_out[...] = out[3 * hid : 3 * hid + 1, :]
    gb2_out[...] = out[3 * hid + 1 : 3 * hid + 2, :]
    gg_out[...] = out[3 * hid + 2 : 3 * hid + 3, :]
    for copy in sends:
        copy.wait_send()


def finish_kernel(*refs):
    count = (len(refs) - 1) // 2
    sem = refs[-1]
    copies = [pltpu.make_async_copy(refs[i], refs[count + i], sem.at[i]) for i in range(count)]
    for copy in copies:
        copy.start()
    for copy in copies:
        copy.wait()


def shards(
    node_state, w_msg, w_first, b_first, w_second, b_second, ln_gain, col_index, edge_counts, cotangent
):
    rows, hid = node_state.shape
    nb, tiles, blk, _ = edge_counts.shape
    ext = rows + 2 * WIN * blk
    devices = lax.axis_size("dom") * lax.axis_size("feat")
    scale = 1.0 / math.sqrt(rows * devices)
    f32, bf16 = jnp.float32, jnp.bfloat16
    vmem, sem = pltpu.VMEM, pltpu.SemaphoreType.DMA
    in_hbm = pl.BlockSpec(memory_space=pltpu.HBM)
    whole = pl.BlockSpec(memory_space=pltpu.VMEM)
    shape = jax.ShapeDtypeStruct
    row = shape((1, hid), f32)
    results = (
        shape((rows, hid), bf16), shape((rows, hid), bf16), shape((hid, hid), f32),
        shape((2 * hid, hid), f32), row, shape((hid, hid), f32), row, row,
    )
    results = pl.pallas_call(
        functools.partial(layer_kernel, scale),
        out_shape=results,
        in_specs=[in_hbm] * 10,
        out_specs=(whole,) * 8,
        scratch_shapes=[
            vmem((ext, hid), bf16), vmem((hid, hid), bf16), vmem((hid, hid), bf16), vmem((2 * hid, hid), bf16), vmem((1, hid), f32),
            vmem((hid, hid), bf16), vmem((1, hid), f32), vmem((1, hid), f32), pltpu.SMEM((tiles, nb), jnp.int32),
            vmem((nb, tiles, blk, blk), jnp.int32), vmem((rows, hid), bf16),
            vmem((nb, blk, SPAN * blk), bf16), vmem((rows, hid), bf16), vmem((rows, hid), f32), vmem((ext, hid), f32),
            vmem((TOTAL, hid), f32), vmem((NX, QUARTER, hid), f32), vmem((NX, QUARTER, hid), f32),
            vmem((NX - 1, QUARTER, hid), f32), vmem((QUARTER, hid), f32), vmem((NY - 1, PIECE, hid), f32),
            vmem((PIECE, hid), f32), vmem((NZ, PIECE, hid), f32), vmem((TOTAL, hid), f32),
            vmem((2, WIN * blk, hid), bf16), vmem((2, WIN * blk, hid), bf16),
            sem((9,)), sem((nb,)), sem((2,)), sem((2,)), sem((4,)), sem((4,)), sem((3,)), sem((3,)),
            sem((7,)), sem((7,)), sem((11,)), sem((11,)), sem((7,)), sem((7,)), sem((3,)), sem((3,)),
            sem((4,)), sem((4,)), sem((2,)), sem((2,)),
        ],
        compiler_params=pltpu.CompilerParams(
            collective_id=0, has_side_effects=True, vmem_limit_bytes=32 * 1024 * 1024
        ),
        name="layer",
    )(
        *[
            pltpu.with_memory_space_constraint(a, pltpu.HBM)
            for a in (
                node_state, w_msg, w_first, b_first.reshape(1, hid), w_second, b_second.reshape(1, hid),
                ln_gain.reshape(1, hid), col_index.T, edge_counts, cotangent,
            )
        ]
    )
    upd, gs, gwm, gwf, gb1, gws, gb2, gg = pl.pallas_call(
        finish_kernel,
        out_shape=tuple(shape(r.shape, r.dtype) for r in results),
        in_specs=[whole] * 8,
        out_specs=(in_hbm,) * 8,
        scratch_shapes=[sem((8,))],
        compiler_params=pltpu.CompilerParams(vmem_limit_bytes=4 * 1024 * 1024),
        name="finish",
    )(*results)
    return (upd, gs, gwm, gwf, gb1.reshape(hid), gws, gb2.reshape(hid), gg.reshape(hid))


def solution(mesh):
    nodes = P(("dom", "feat"), None)
    return jax.shard_map(
        shards,
        mesh=mesh,
        in_specs=(nodes, P(), P(), P(), P(), P(), P(), nodes, P(("dom", "feat"), None, None, None), nodes),
        out_specs=(nodes, nodes, P(), P(), P(), P(), P(), P()),
        check_vma=False,
    )
```

```python
import functools
import math

import jax
import jax.numpy as jnp
from jax import lax
from jax.experimental import pallas as pl
from jax.experimental.pallas import tpu as pltpu
from jax.sharding import PartitionSpec as P

MESH = pl.DeviceIdType.MESH
WIN = 2
SPAN = 2 * WIN + 1
EPS = 1e-05
NX, NY, NZ, Z_LO, CORES = 4, 8, 12, 4, 2
PIECE = 8
QUARTER = PIECE * NY
HALF = QUARTER * NX
TOTAL = HALF * CORES
GROUP = 2


def dot(a, b):
    return jnp.dot(a, b, preferred_element_type=jnp.float32)


def dot_rt(a, b):
    return lax.dot_general(a, b, (((1,), (1,)), ((), ())), preferred_element_type=jnp.float32)


def dot_lt(a, b):
    return lax.dot_general(a, b, (((0,), (0,)), ((), ())), preferred_element_type=jnp.float32)


def layer_kernel(
    scale,
    x_hbm, wmsg_hbm, wf_hbm, bf_hbm, ws_hbm, bs_hbm, gain_hbm, col_hbm, cnt_hbm, cot_hbm,
    upd_out, gs_out, gwm_out, gwf_out, gb1_out, gws_out, gb2_out, gg_out,
    xe, wmsg, wmsg_t, wf, bf, ws, bs, gain, col, cnt, cot,
    band, dag, gsp, dme, pay, pay_b, r1, a1, r2, a2, a2_b, r3, a3, r4, out, bh_send, bh_recv,
    in_sem, cnt_sem, halo_s, halo_r, c_s, c_r, x_s, x_r, y_s, y_r, z_s, z_r,
    ay_s, ay_r, ax_s, ax_r, ac_s, ac_r, b_s, b_r,
):
    nb = cnt_hbm.shape[0]
    hid = x_hbm.shape[1]
    rows = x_hbm.shape[0]
    blk = cnt_hbm.shape[2]
    edge = WIN * blk
    ndom, nfeat = lax.axis_size("dom"), lax.axis_size("feat")
    count = ndom * nfeat
    dom, feat = lax.axis_index("dom"), lax.axis_index("feat")
    core, z_lo, y = lax.rem(dom, CORES), lax.rem(dom // CORES, Z_LO), dom // (CORES * Z_LO)
    x, z_hi = lax.rem(feat, NX), feat // NX
    z = z_hi * Z_LO + z_lo
    rank = dom * nfeat + feat
    first_block = rank * nb

    def by_rank(r):
        return (r // nfeat, lax.rem(r, nfeat))

    nxt = by_rank(lax.rem(rank + 1, count))
    prv = by_rank(lax.rem(rank + count - 1, count))
    mate = (dom + 1 - 2 * core, feat)

    def at_x(k):
        return (dom, z_hi * NX + lax.rem(x + k, NX))

    def at_y(k):
        return ((lax.rem(y + k, NY) * Z_LO + z_lo) * CORES + core, feat)

    def at_z(k):
        other = lax.rem(z + k, NZ)
        return ((y * Z_LO + lax.rem(other, Z_LO)) * CORES + core, (other // Z_LO) * NX + x)

    peers = [prv, nxt]
    peers += [at_z(k) for k in (6, 5, 7, 4, 8, 3, 9, 2, 10, 1, 11)]
    peers += [at_y(k) for k in range(1, NY)]
    peers += [at_x(k) for k in range(1, NX)]
    peers += [mate]
    barrier = pltpu.get_barrier_semaphore()
    for peer in peers:
        pl.semaphore_signal(barrier, inc=1, device_id=peer, device_id_type=MESH)

    loads = [
        pltpu.make_async_copy(src, dst, in_sem.at[i])
        for i, (src, dst) in enumerate(
            (
                (col_hbm, col),
                (x_hbm, xe.at[pl.ds(edge, rows)]),
                (cot_hbm, cot),
                (wmsg_hbm, wmsg),
                (wf_hbm, wf),
                (bf_hbm, bf),
                (ws_hbm, ws),
                (bs_hbm, bs),
                (gain_hbm, gain),
            )
        )
    ]
    cnt_loads = [pltpu.make_async_copy(cnt_hbm.at[b], cnt.at[b], cnt_sem.at[b]) for b in range(nb)]
    loads[0].start()
    for b in range(nb):
        cnt_loads[b].start()
    for load in loads[1:]:
        load.start()

    pay[...] = jnp.zeros_like(pay)
    dme[...] = jnp.zeros_like(dme)
    loads[0].wait()

    def build(b, carry):
        pltpu.make_async_copy(cnt_hbm.at[b], cnt.at[b], cnt_sem.at[b]).wait()
        tiles = [cnt[b, t].astype(jnp.float32).astype(jnp.bfloat16) for t in range(cnt.shape[1])]
        for d in range(SPAN):
            acc = tiles[0] if d == WIN else None
            for t in range(1, cnt.shape[1]):
                here = (col[t, b] - first_block - b + WIN == d).astype(jnp.float32)
                term = tiles[t] * jnp.full((blk, blk), here, jnp.float32).astype(jnp.bfloat16)
                acc = term if acc is None else acc + term
            band[b, :, d * blk : (d + 1) * blk] = acc
        return carry

    lax.fori_loop(0, nb, build, 0)
    pl.semaphore_wait(barrier, len(peers))

    halo_low = pltpu.make_async_remote_copy(
        src_ref=x_hbm.at[pl.ds(0, edge)], dst_ref=xe.at[pl.ds(edge + rows, edge)],
        send_sem=halo_s.at[0], recv_sem=halo_r.at[0], device_id=prv, device_id_type=MESH,
    )
    halo_high = pltpu.make_async_remote_copy(
        src_ref=x_hbm.at[pl.ds(rows - edge, edge)], dst_ref=xe.at[pl.ds(0, edge)],
        send_sem=halo_s.at[1], recv_sem=halo_r.at[1], device_id=nxt, device_id_type=MESH,
    )
    halo_low.start()
    halo_high.start()
    for load in loads[1:]:
        load.wait()

    wmsg_t[...] = wmsg[...].T
    size = GROUP * blk

    def process(b0):
        r0 = pl.multiple_of(b0 * blk, blk)
        here = pl.ds(r0, size)
        xs = xe[pl.ds(r0 + edge, size), :]
        agx = jnp.concatenate(
            [dot(band[b0 + g], xe[pl.ds(r0 + g * blk, SPAN * blk), :]) for g in range(GROUP)], axis=0
        ).astype(jnp.bfloat16)
        agg = dot(agx, wmsg[...]).astype(jnp.bfloat16)
        ph = dot(jnp.concatenate([xs, agg], axis=1), wf[...]) + bf[...]
        sg = jax.nn.sigmoid(ph)
        act = (ph * sg).astype(jnp.bfloat16)
        pn = dot(act, ws[...]) + bs[...]
        cen = pn - jnp.mean(pn, axis=-1, keepdims=True)
        inv = lax.rsqrt(jnp.mean(cen * cen, axis=-1, keepdims=True) + EPS)
        nrm = cen * inv
        upd_out[here, :] = (xs.astype(jnp.float32) + gain[...] * nrm).astype(jnp.bfloat16)
        c = cot[here, :].astype(jnp.float32)
        q = c * gain[...]
        dpn = (
            inv
            * (
                q
                - jnp.mean(q, axis=-1, keepdims=True)
                - nrm * jnp.mean(q * nrm, axis=-1, keepdims=True)
            )
        ).astype(jnp.bfloat16)
        dph = (dot_rt(dpn, ws[...]) * sg * (1.0 + ph * (1.0 - sg))).astype(jnp.bfloat16)
        dj = dot_rt(dph, wf[...])
        gsp[here, :] = c + dj[:, :blk]
        dag[here, :] = dj[:, blk:].astype(jnp.bfloat16)
        pay[0:blk, :] += dot_lt(xs, dph)
        pay[blk : 2 * blk, :] += dot_lt(agx, dph)
        pay[2 * blk : 3 * blk, :] += dot_lt(act, dpn)
        pay[3 * blk : 3 * blk + 1, :] += jnp.sum(dph.astype(jnp.float32), axis=0, keepdims=True)
        pay[3 * blk + 1 : 3 * blk + 2, :] += jnp.sum(dpn.astype(jnp.float32), axis=0, keepdims=True)
        pay[3 * blk + 2 : 3 * blk + 3, :] += jnp.sum(c * nrm, axis=0, keepdims=True)

    def interior(i, carry):
        process(WIN + GROUP * i)
        return carry

    lax.fori_loop(0, (nb - 2 * WIN) // GROUP, interior, 0)
    halo_low.wait_recv()
    halo_high.wait_recv()

    def border(i, carry):
        process(i * (nb - WIN))
        return carry

    lax.fori_loop(0, 2, border, 0)

    order = (2, 1, 3, 0)
    quarters = [lax.rem(x + off, NX) for off in order]
    pay_b[...] = pay[...].astype(jnp.bfloat16)
    to_mate = []
    for j, q in enumerate(quarters):
        to_mate.append(
            pltpu.make_async_remote_copy(
                src_ref=pay_b.at[pl.ds(pl.multiple_of((1 - core) * HALF + q * QUARTER, QUARTER), QUARTER)],
                dst_ref=r1.at[j], send_sem=c_s.at[j], recv_sem=c_r.at[j], device_id=mate, device_id_type=MESH,
            )
        )
        to_mate[-1].start()

    def scatter_row(b):
        r0 = pl.multiple_of(b * blk, blk)
        dme[pl.ds(r0, SPAN * blk), :] += dot_lt(band[b], dag[pl.ds(r0, blk), :])

    sends = list(to_mate)
    along_x = []
    for j, q in enumerate(quarters):
        to_mate[j].wait_recv()
        mine = pay[pl.ds(pl.multiple_of(core * HALF + q * QUARTER, QUARTER), QUARTER), :]
        part = mine + r1[j].astype(jnp.float32)
        off = order[j]
        if off:
            a1[j] = part.astype(jnp.bfloat16)
            copy = pltpu.make_async_remote_copy(
                src_ref=a1.at[j], dst_ref=r2.at[j],
                send_sem=x_s.at[j], recv_sem=x_r.at[j], device_id=at_x(off), device_id_type=MESH,
            )
            copy.start()
            along_x.append(copy)
    sends += along_x

    def border_rows(i, carry):
        b0 = i * (nb - WIN)
        for g in range(WIN):
            scatter_row(b0 + g)
        return carry

    lax.fori_loop(0, 2, border_rows, 0)
    bh_send[0] = dme[0:edge, :].astype(jnp.bfloat16)
    bh_send[1] = dme[edge + rows : 2 * edge + rows, :].astype(jnp.bfloat16)
    back_low = pltpu.make_async_remote_copy(
        src_ref=bh_send.at[0], dst_ref=bh_recv.at[0],
        send_sem=b_s.at[0], recv_sem=b_r.at[0], device_id=prv, device_id_type=MESH,
    )
    back_high = pltpu.make_async_remote_copy(
        src_ref=bh_send.at[1], dst_ref=bh_recv.at[1],
        send_sem=b_s.at[1], recv_sem=b_r.at[1], device_id=nxt, device_id_type=MESH,
    )
    back_low.start()
    back_high.start()
    sends += [halo_low, halo_high, back_low, back_high]

    for copy in along_x:
        copy.wait_recv()
    part = part + (r2[0].astype(jnp.float32) + (r2[1].astype(jnp.float32) + r2[2].astype(jnp.float32)))
    part = part.reshape(NY, PIECE, hid)
    a2[...] = part
    a2_b[...] = part.astype(jnp.bfloat16)
    along_y = []
    for k in range(1, NY):
        copy = pltpu.make_async_remote_copy(
            src_ref=a2_b.at[lax.rem(y + k, NY)],
            dst_ref=r3.at[k - 1],
            send_sem=y_s.at[k - 1], recv_sem=y_r.at[k - 1], device_id=at_y(k), device_id_type=MESH,
        )
        copy.start()
        along_y.append(copy)
    sends += along_y

    def inner_rows(b, carry):
        scatter_row(b)
        return carry

    lax.fori_loop(WIN, nb - WIN, inner_rows, 0)

    for copy in along_y:
        copy.wait_recv()
    total = a2[y]
    for k in range(1, NY):
        total = total + r3[k - 1].astype(jnp.float32)
    total = (total * scale).astype(jnp.bfloat16)
    a3[...] = total
    r4[z] = total
    along_z = []
    for k in (6, 5, 7, 4, 8, 3, 9, 2, 10, 1, 11):
        copy = pltpu.make_async_remote_copy(
            src_ref=a3, dst_ref=r4.at[z],
            send_sem=z_s.at[k - 1], recv_sem=z_r.at[k - 1], device_id=at_z(k), device_id_type=MESH,
        )
        copy.start()
        along_z.append(copy)
    sends += along_z

    back_low.wait_recv()
    back_high.wait_recv()
    dme[edge : 2 * edge, :] += bh_recv[1].astype(jnp.float32)
    dme[rows : rows + edge, :] += bh_recv[0].astype(jnp.float32)

    def state_rows(i, carry):
        r0 = pl.multiple_of(i * size, size)
        here = pl.ds(r0, size)
        dm = dme[pl.ds(r0 + edge, size), :].astype(jnp.bfloat16)
        gs_out[here, :] = (gsp[here, :] + dot_rt(dm, wmsg[...])).astype(jnp.bfloat16)
        return carry

    lax.fori_loop(0, rows // size, state_rows, 0)

    for copy in along_z:
        copy.wait_recv()
    total = r4[0].astype(jnp.float32)
    for i in range(1, NZ):
        total = total + r4[i].astype(jnp.float32)
    half0 = core * (NX * NY)
    quarter0 = half0 + x * NY
    own = quarter0 + y
    out[own] = total.astype(jnp.bfloat16)
    gathers = []
    for k in range(1, NY):
        copy = pltpu.make_async_remote_copy(
            src_ref=out.at[own], dst_ref=out.at[own],
            send_sem=ay_s.at[k - 1], recv_sem=ay_r.at[k - 1], device_id=at_y(k), device_id_type=MESH,
        )
        copy.start()
        gathers.append(copy)
    for copy in gathers:
        copy.wait_recv()
    sends += gathers
    span = pl.ds(quarter0, NY)
    along_x = []
    for j, k in enumerate((2, 1, 3)):
        copy = pltpu.make_async_remote_copy(
            src_ref=out.at[span], dst_ref=out.at[span],
            send_sem=ax_s.at[j], recv_sem=ax_r.at[j], device_id=at_x(k), device_id_type=MESH,
        )
        copy.start()
        along_x.append(copy)
    sends += along_x
    shares = []
    for j, k in enumerate((0, 1, 3, 2)):
        if k:
            along_x[(2, 1, 3).index(k)].wait_recv()
        span = pl.ds(half0 + lax.rem(x + NX - k, NX) * NY, NY)
        copy = pltpu.make_async_remote_copy(
            src_ref=out.at[span], dst_ref=out.at[span],
            send_sem=ac_s.at[j], recv_sem=ac_r.at[j], device_id=mate, device_id_type=MESH,
        )
        copy.start()
        shares.append(copy)
    sends += shares
    for copy in shares:
        copy.wait_recv()
    total = out[...].astype(jnp.float32).reshape(TOTAL, hid)
    grad_s = total[hid : 2 * hid].astype(jnp.bfloat16)
    gwm_out[...] = dot_rt(grad_s, wf[hid:, :])
    gwf_out[0:hid, :] = total[0:hid]
    gwf_out[hid:, :] = dot(wmsg_t[...], grad_s)
    gws_out[...] = total[2 * hid : 3 * hid]
    gb1_out[...] = total[3 * hid : 3 * hid + 1]
    gb2_out[...] = total[3 * hid + 1 : 3 * hid + 2]
    gg_out[...] = total[3 * hid + 2 : 3 * hid + 3]
    for copy in sends:
        copy.wait_send()


def finish_kernel(*refs):
    count = (len(refs) - 1) // 2
    sem = refs[-1]
    copies = [pltpu.make_async_copy(refs[i], refs[count + i], sem.at[i]) for i in range(count)]
    for copy in copies:
        copy.start()
    for copy in copies:
        copy.wait()


def shards(
    node_state, w_msg, w_first, b_first, w_second, b_second, ln_gain, col_index, edge_counts, cotangent
):
    rows, hid = node_state.shape
    nb, tiles, blk, _ = edge_counts.shape
    ext = rows + 2 * WIN * blk
    devices = lax.axis_size("dom") * lax.axis_size("feat")
    scale = 1.0 / math.sqrt(rows * devices)
    f32, bf16 = jnp.float32, jnp.bfloat16
    vmem, sem = pltpu.VMEM, pltpu.SemaphoreType.DMA
    in_hbm = pl.BlockSpec(memory_space=pltpu.HBM)
    whole = pl.BlockSpec(memory_space=pltpu.VMEM)
    shape = jax.ShapeDtypeStruct
    row = shape((1, hid), f32)
    results = (
        shape((rows, hid), bf16), shape((rows, hid), bf16), shape((hid, hid), f32),
        shape((2 * hid, hid), f32), row, shape((hid, hid), f32), row, row,
    )
    results = pl.pallas_call(
        functools.partial(layer_kernel, scale),
        out_shape=results,
        in_specs=[in_hbm] * 10,
        out_specs=(whole,) * 8,
        scratch_shapes=[
            vmem((ext, hid), bf16), vmem((hid, hid), bf16), vmem((hid, hid), bf16), vmem((2 * hid, hid), bf16), vmem((1, hid), f32),
            vmem((hid, hid), bf16), vmem((1, hid), f32), vmem((1, hid), f32), pltpu.SMEM((tiles, nb), jnp.int32),
            vmem((nb, tiles, blk, blk), jnp.int32), vmem((rows, hid), bf16),
            vmem((nb, blk, SPAN * blk), bf16), vmem((rows, hid), bf16), vmem((rows, hid), f32), vmem((ext, hid), f32),
            vmem((TOTAL, hid), f32), vmem((TOTAL, hid), bf16), vmem((NX, QUARTER, hid), bf16),
            vmem((NX, QUARTER, hid), bf16), vmem((NX - 1, QUARTER, hid), bf16), vmem((NY, PIECE, hid), f32),
            vmem((NY, PIECE, hid), bf16), vmem((NY - 1, PIECE, hid), bf16), vmem((PIECE, hid), bf16),
            vmem((NZ, PIECE, hid), bf16), vmem((TOTAL // PIECE, PIECE, hid), bf16),
            vmem((2, WIN * blk, hid), bf16), vmem((2, WIN * blk, hid), bf16),
            sem((9,)), sem((nb,)), sem((2,)), sem((2,)), sem((4,)), sem((4,)), sem((3,)), sem((3,)),
            sem((7,)), sem((7,)), sem((11,)), sem((11,)), sem((7,)), sem((7,)), sem((3,)), sem((3,)),
            sem((4,)), sem((4,)), sem((2,)), sem((2,)),
        ],
        compiler_params=pltpu.CompilerParams(
            collective_id=0, has_side_effects=True, vmem_limit_bytes=32 * 1024 * 1024
        ),
        name="layer",
    )(
        *[
            pltpu.with_memory_space_constraint(a, pltpu.HBM)
            for a in (
                node_state, w_msg, w_first, b_first.reshape(1, hid), w_second, b_second.reshape(1, hid),
                ln_gain.reshape(1, hid), col_index.T, edge_counts, cotangent,
            )
        ]
    )
    upd, gs, gwm, gwf, gb1, gws, gb2, gg = pl.pallas_call(
        finish_kernel,
        out_shape=tuple(shape(r.shape, r.dtype) for r in results),
        in_specs=[whole] * 8,
        out_specs=(in_hbm,) * 8,
        scratch_shapes=[sem((8,))],
        compiler_params=pltpu.CompilerParams(vmem_limit_bytes=4 * 1024 * 1024),
        name="finish",
    )(*results)
    return (upd, gs, gwm, gwf, gb1.reshape(hid), gws, gb2.reshape(hid), gg.reshape(hid))


def solution(mesh):
    nodes = P(("dom", "feat"), None)
    return jax.shard_map(
        shards,
        mesh=mesh,
        in_specs=(nodes, P(), P(), P(), P(), P(), P(), nodes, P(("dom", "feat"), None, None, None), nodes),
        out_specs=(nodes, nodes, P(), P(), P(), P(), P(), P()),
        check_vma=False,
    )
```
